1024 devices in a mesh: dp: 32 (over z, core), group: 4 (over x), tensor: 8 (over y).
Axes of the slice: x: 4, y: 8, z: 16, core: 2. Of those that a mesh axis runs over, the one named last changes fastest.
Arguments:
- attn_heads: bfloat16 [8192, 8192], P('dp', ('group', 'tensor')), parts along dimension 0, may hold values from -6 to 6
- out_proj: bfloat16 [8192, 3584], P(('group', 'tensor')), may hold values from -0.0625 to 0.0625
- residual_in: bfloat16 [8192, 3584], P(('dp', 'group', 'tensor')), parts along dimension 0, may hold values from -6 to 6
- norm_gain: float32 [3584], replicated, may hold values from 0.1 to 1.9
- expert_ids: int32 [8192, 4], P(('dp', 'group', 'tensor')), parts along dimension 0, may hold values from 0 to 7, as said below
- gate_weights: bfloat16 [8192, 4], P(('dp', 'group', 'tensor')), parts along dimension 0, may hold values from 0.19921875 to 1.5
- w_gate: bfloat16 [8, 3584, 1024], P('group', None, 'tensor'), may hold values from -0.09375 to 0.09375
- w_up: bfloat16 [8, 3584, 1024], P('group', None, 'tensor'), may hold values from -0.09375 to 0.09375
- w_down: bfloat16 [8, 1024, 3584], P('group', 'tensor'), may hold values from -0.1875 to 0.1875
Outputs:
- layer_out: bfloat16 [8192, 3584], P(('dp', 'group', 'tensor')), parts along dimension 0
The draws below stay inside these ranges and needn't reach their ends.
There are 32 independent parts, one for each index of `dp`. The reference program is written for one: setup_inputs(seed, part) draws one part's arguments, and reference() takes and returns one part's arrays. A program takes and returns all parts, laid end to end along the dimension named above; an argument that names none is the same for every part. Nothing has to cross between parts.
Inputs may be any that keep to these rules, and one draw needn't show every extreme that they name: `expert_ids`: each row names 4 different experts, of at most 3 node groups (expert e belongs to node group e // 2). In each aligned block of 8 rows (the rows of one device) at most 6 rows name experts of any one node group, and in every draw some node group is named by exactly 6 rows of every block.
All inputs are finite; a program needn't handle non-finite values.
Results may differ from the reference program's by a relative error of at most 0.02.
Values may be sent and summed in bfloat16 or wider, within the bound.
No kernel may reach another device: no remote copies, remote signals or barrier semaphores. Data moves between devices by JAX's collectives and lax.ppermute only.
A program may use at most 64 MiB of HBM per device.

```python
import jax
import jax.numpy as jnp
from jax import lax

D = 3584
FFE = 1024
EXP_NODE = 2
TOPK = 4
TOK_DEV = 8
HDH = 8192
TOKENS = 256
EXPERTS = 8
N_GROUP = 4
N_TENSOR = 8


def draw_expert_ids(key, part):
    blocks = TOKENS // TOK_DEV
    subkeys = jax.random.split(jax.random.fold_in(key, 11), 7)
    groups = jnp.arange(4, dtype=jnp.int32)
    rank_scores = jax.random.randint(subkeys[0], (blocks, TOK_DEV), 0, 1 << 20) * TOK_DEV + jnp.arange(TOK_DEV, dtype=jnp.int32)[None, :]
    permuted = jnp.argsort(rank_scores, axis=1).astype(jnp.int32)
    excluded = permuted % 4
    full_group = jax.random.randint(subkeys[1], (1, 1, 1), 0, 4)
    candidate = (groups[None, None, :] != excluded[:, :, None]) & (groups[None, None, :] != full_group)
    scores = jax.random.randint(subkeys[2], (blocks, TOK_DEV, 4), 1, 1 << 20) * 4 + groups[None, None, :]
    second = jnp.argmax(jnp.where(candidate, scores, -1), axis=2).astype(jnp.int32)
    dropping = jax.random.randint(subkeys[3], (blocks, TOK_DEV, 1), 0, 2)
    group_used = (groups[None, None, :] != excluded[:, :, None]) & jnp.logical_not((dropping == 1) & (groups[None, None, :] == second[:, :, None]))
    double_scores = jax.random.randint(subkeys[4], (blocks, TOK_DEV, 4), 1, 1 << 20) * 4 + groups[None, None, :]
    doubled = jnp.argmax(jnp.where(group_used, double_scores, -1), axis=2).astype(jnp.int32)
    used_count = jnp.sum(group_used.astype(jnp.int32), axis=2, keepdims=True)
    takes_both = group_used & ((used_count == 2) | (groups[None, None, :] == doubled[:, :, None]))
    expert_bit = jax.random.randint(subkeys[5], (blocks, TOK_DEV, 4), 0, 2)
    take_first = takes_both | group_used & (expert_bit == 0)
    take_second = takes_both | group_used & (expert_bit == 1)
    expert_flags = jnp.stack([take_first, take_second], axis=3).reshape(blocks, TOK_DEV, 8)
    sort_keys = jnp.where(expert_flags, 0, 8) + jnp.arange(8, dtype=jnp.int32)[None, None, :]
    chosen = jnp.argsort(sort_keys, axis=2)[:, :, :TOPK].astype(jnp.int32)
    mix_scores = jax.random.randint(subkeys[6], (blocks, TOK_DEV, TOPK), 0, 1 << 20) * TOPK + jnp.arange(TOPK, dtype=jnp.int32)[None, None, :]
    mixing = jnp.argsort(mix_scores, axis=2)
    chosen = jnp.take_along_axis(chosen, mixing, axis=2)
    return chosen.reshape(TOKENS, TOPK).astype(jnp.int32)


def steps_of(stream_key, shape, shards, smallest, top_value):
    factor_of = 1.0
    for dim, blocks in shards:
        heights = jax.random.uniform(jax.random.fold_in(jax.random.fold_in(stream_key, 6), dim), (blocks,), jnp.float32, smallest / len(shards), top_value / len(shards))
        factor_of = factor_of * jnp.repeat(jnp.exp(heights), shape[dim] // blocks).reshape((-1,) + (1,) * (len(shape) - 1 - dim))
    return factor_of


def noise(rng, shape, scale, most, cuts=(), held_as=jnp.bfloat16):
    factor_of = steps_of(rng, shape, cuts, -0.22, 0.18) if cuts else 1.0
    drawn = jax.random.normal(rng, shape, jnp.float32) * scale * factor_of
    return jnp.minimum(jnp.maximum(drawn, -most), most).astype(held_as)


def setup_inputs(seed: int = 0, part: int = 0) -> dict:
    splits = jax.random.split(jax.random.key(seed), 10)
    part_keys = jax.random.split(jax.random.fold_in(splits[9], part), 10)
    return {
        "attn_heads": noise(part_keys[0], (TOKENS, HDH), 1.0, 6.0, ((1, 32),)),
        "out_proj": noise(splits[1], (HDH, D), HDH ** -0.5, 0.0625, ((0, 32),)),
        "residual_in": noise(part_keys[2], (TOKENS, D), 1.0, 6.0, ((0, 32),)),
        "norm_gain": jnp.clip(1.0 + 0.18 * jax.random.normal(splits[3], (D,), jnp.float32), 0.1, 1.9),
        "expert_ids": draw_expert_ids(jax.random.fold_in(jax.random.fold_in(splits[9], part), 71), part),
        "gate_weights": jnp.clip(0.19921875 + 1.3007812 * jax.random.uniform(part_keys[5], (TOKENS, TOPK), jnp.float32) ** steps_of(part_keys[5], (TOKENS, TOPK), ((0, 32),), -0.2, 0.2), 0.19921875, 1.5).astype(jnp.bfloat16),
        "w_gate": noise(splits[6], (EXPERTS, D, FFE), D ** -0.5, 0.09375, ((0, 4), (2, 8))),
        "w_up": noise(splits[7], (EXPERTS, D, FFE), D ** -0.5, 0.09375, ((0, 4), (2, 8))),
        "w_down": noise(splits[8], (EXPERTS, FFE, D), FFE ** -0.5, 0.1875, ((0, 4), (1, 8))),
    }


def reference(attn_heads, out_proj, residual_in, norm_gain, expert_ids, gate_weights, w_gate, w_up, w_down):
    projected = jnp.dot(attn_heads, out_proj, preferred_element_type=jnp.float32).astype(jnp.bfloat16)
    hidden = (residual_in.astype(jnp.float32) + projected.astype(jnp.float32)).astype(jnp.bfloat16)
    stream = hidden.astype(jnp.float32)
    scale = lax.rsqrt(lax.optimization_barrier(jnp.mean(stream * stream, axis=1, keepdims=True)) + 1e-06)
    normed = (stream * scale * norm_gain).astype(jnp.bfloat16)
    matches = (expert_ids[:, :, None] == jnp.arange(EXPERTS, dtype=jnp.int32)[None, None, :]).astype(jnp.float32)
    routing = lax.optimization_barrier(jnp.sum(matches * gate_weights.astype(jnp.float32)[:, :, None], axis=1))
    block_width = FFE // N_TENSOR
    mixture = jnp.zeros((TOKENS, D), jnp.float32)
    for node_index in range(N_GROUP):
        activations = []
        for member in range(EXP_NODE):
            expert = node_index * EXP_NODE + member
            gate_proj = jnp.dot(normed, w_gate[expert], preferred_element_type=jnp.float32)
            up_proj = jnp.dot(normed, w_up[expert], preferred_element_type=jnp.float32)
            activations.append((jax.nn.silu(gate_proj) * up_proj).astype(jnp.bfloat16))
        node_sum = jnp.zeros((TOKENS, D), jnp.float32)
        for block_index in range(N_TENSOR):
            low = block_index * block_width
            block_sum = jnp.zeros((TOKENS, D), jnp.float32)
            for member in range(EXP_NODE):
                expert = node_index * EXP_NODE + member
                block_sum = block_sum + routing[:, expert:expert + 1] * jnp.dot(activations[member][:, low:low + block_width], w_down[expert, low:low + block_width, :], preferred_element_type=jnp.float32)
            rounded = lax.optimization_barrier(block_sum.astype(jnp.bfloat16))
            node_sum = node_sum + rounded.astype(jnp.float32)
        node_rounded = lax.optimization_barrier(node_sum.astype(jnp.bfloat16))
        mixture = mixture + node_rounded.astype(jnp.float32)
    return (stream + mixture).astype(jnp.bfloat16)
```

```python
import jax
import jax.numpy as jnp
from jax import lax
from jax.experimental import pallas as pl
from jax.experimental.pallas import tpu as pltpu
from jax.sharding import Mesh, PartitionSpec as P

BF = jnp.bfloat16
F32 = jnp.float32
LANES = 128


def whole(shape):
    return pl.BlockSpec(shape, lambda *_: (0,) * len(shape))


def call(body, outs, grid=None, in_specs=None, out_specs=None, scratch=(), vmem=20 << 20):
    return pl.pallas_call(
        body,
        out_shape=outs,
        grid=grid if grid is not None else (),
        in_specs=in_specs,
        out_specs=out_specs,
        scratch_shapes=scratch,
        compiler_params=pltpu.CompilerParams(vmem_limit_bytes=vmem),
    )


def exchange(blocks, axes):
    return lax.all_to_all(blocks, axes, 0, 0, tiled=True)


def project(attn, weight, groups, quads, pairs, tokens):
    rows, depth = attn.shape
    features = weight.shape[1]
    width = 512

    def body(a_ref, w_ref, o_ref):
        out = jnp.dot(a_ref[...], w_ref[...], preferred_element_type=F32).astype(BF)
        for g in range(groups):
            for p in range(pairs):
                for q in range(quads):
                    src = ((g * quads + q) * pairs + p) * tokens
                    dst = ((g * pairs + p) * quads + q) * tokens
                    o_ref[dst : dst + tokens, :] = out[src : src + tokens, :]

    return call(
        body,
        jax.ShapeDtypeStruct((rows, features), BF),
        grid=(features // width,),
        in_specs=[whole((rows, depth)), pl.BlockSpec((depth, width), lambda j: (0, j))],
        out_specs=pl.BlockSpec((rows, width), lambda j: (0, j)),
    )(attn, weight)


def sum_blocks(blocks):
    count, rows, features = blocks.shape

    def body(x_ref, o_ref):
        total = x_ref[0].astype(F32)
        for s in range(1, count):
            total = total + x_ref[s].astype(F32)
        o_ref[...] = total.astype(BF)

    return call(
        body,
        jax.ShapeDtypeStruct((rows, features), BF),
        in_specs=[pl.BlockSpec(memory_space=pltpu.VMEM)],
        out_specs=pl.BlockSpec(memory_space=pltpu.VMEM),
    )(blocks)


def finish_hidden(parts, residual, gain, ids, gates, copies, experts):
    count, tokens, features = parts.shape

    def body(x_ref, r_ref, g_ref, id_ref, w_ref, h_ref, o_ref):
        total = x_ref[0].astype(F32)
        for s in range(1, count):
            total = total + x_ref[s].astype(F32)
        projected = total.astype(BF).astype(F32)
        hidden = (r_ref[...].astype(F32) + projected).astype(BF)
        h_ref[...] = hidden
        stream = hidden.astype(F32)
        scale = lax.rsqrt(jnp.mean(stream * stream, axis=1, keepdims=True) + 1e-06)
        normed = (stream * scale * g_ref[...]).astype(BF)
        lane = lax.broadcasted_iota(jnp.int32, (tokens, LANES), 1)
        table = jnp.zeros((tokens, LANES), F32)
        picks = id_ref[...]
        gate = w_ref[...].astype(F32)
        for k in range(picks.shape[1]):
            table = table + jnp.where(lane == picks[:, k : k + 1], gate[:, k : k + 1], 0.0)
        table = table.astype(BF)
        for s in range(copies):
            o_ref[s, :, :features] = normed
            o_ref[s, :, features:] = table

    return call(
        body,
        (
            jax.ShapeDtypeStruct((tokens, features), BF),
            jax.ShapeDtypeStruct((copies, tokens, features + LANES), BF),
        ),
        in_specs=[pl.BlockSpec(memory_space=pltpu.VMEM)] * 5,
        out_specs=(pl.BlockSpec(memory_space=pltpu.VMEM),) * 2,
    )(parts, residual, gain, ids, gates)


def slot_of(index, slots):
    block = (index * 171) >> 10 if slots == 6 else index // slots
    return block, index - block * slots


def one_hot(table, table_first, groups, quads, repeat, tokens, slots):
    here = quads * tokens
    there = groups * repeat * quads * slots
    members = 2

    def split(index):
        block, slot = slot_of(index, slots)
        quad = block % quads
        group = block // (quads * repeat)
        return group, quad, slot

    group_e, _, _ = split(lax.broadcasted_iota(jnp.int32, (there, LANES), 0))
    expert = lax.broadcasted_iota(jnp.int32, (there, LANES), 1)
    belongs = (expert // members == group_e).astype(BF)
    shape = (here, there) if table_first else (there, here)
    t_dim, s_dim = (0, 1) if table_first else (1, 0)
    nt = (((1,), (1,)), ((), ()))
    pair = (table, belongs) if table_first else (belongs, table)
    chosen = lax.dot_general(*pair, nt, preferred_element_type=F32) > 0
    chosen = jnp.where(chosen, 1.0, 0.0)
    a = lax.broadcasted_iota(jnp.int32, (here, here), 0)
    b = lax.broadcasted_iota(jnp.int32, (here, here), 1)
    row, col = (a, b) if table_first else (b, a)
    before = jnp.where((row // tokens == col // tokens) & (col < row), 1.0, 0.0).astype(BF)
    flag = chosen.astype(BF)
    if table_first:
        position = jnp.dot(before, flag, preferred_element_type=F32)
    else:
        position = jnp.dot(flag, before, preferred_element_type=F32)
    _, quad, slot = split(lax.broadcasted_iota(jnp.int32, shape, s_dim))
    token = lax.broadcasted_iota(jnp.int32, shape, t_dim)
    hit = (token // tokens == quad) & (position == slot.astype(F32))
    return jnp.where(hit, chosen, 0.0).astype(BF)


def pick_rows(seen, groups, quads, pairs, tokens, slots):
    here, wide = seen.shape
    features = wide - LANES
    span = quads * slots

    def body(x_ref, o_ref, t_ref):
        table = x_ref[:, features:]
        t_ref[...] = table
        hot = one_hot(table, False, groups, quads, 1, tokens, slots)
        picked = jnp.dot(hot, x_ref[...], preferred_element_type=F32).astype(BF)
        for g in range(groups):
            for p in range(pairs):
                at = (g * pairs + p) * span
                o_ref[at : at + span, :] = picked[g * span : (g + 1) * span, :]

    return call(
        body,
        (
            jax.ShapeDtypeStruct((groups * pairs * span, wide), BF),
            jax.ShapeDtypeStruct((here, LANES), BF),
        ),
        in_specs=[pl.BlockSpec(memory_space=pltpu.VMEM)],
        out_specs=(pl.BlockSpec(memory_space=pltpu.VMEM),) * 2,
    )(seen)


def experts_of(rows, w_gate, w_up, w_down, group):
    count, wide = rows.shape
    features = wide - LANES
    members, _, units = w_gate.shape

    def body(g_ref, x_ref, wg_ref, wu_ref, wd_ref, o_ref):
        table = x_ref[:, features:].astype(F32)
        lane = lax.broadcasted_iota(jnp.int32, (count, LANES), 1)
        x = x_ref[:, :features]
        acts = []
        for m in range(members):
            gate = jnp.dot(x, wg_ref[m], preferred_element_type=F32)
            up = jnp.dot(x, wu_ref[m], preferred_element_type=F32)
            act = (gate / (1.0 + jnp.exp(-gate)) * up).astype(BF)
            acts.append(act)
        weights = [
            jnp.sum(jnp.where(lane == g_ref[0] * members + m, table, 0.0), axis=1, keepdims=True)
            for m in range(members)
        ]
        step = 512
        for at in range(0, features, step):
            total = jnp.zeros((count, step), F32)
            for m in range(members):
                total = total + weights[m] * jnp.dot(
                    acts[m], wd_ref[m, :, at : at + step], preferred_element_type=F32
                )
            o_ref[:, at : at + step] = total.astype(BF)

    return call(
        body,
        jax.ShapeDtypeStruct((count, features), BF),
        in_specs=[pl.BlockSpec(memory_space=pltpu.SMEM)]
        + [pl.BlockSpec(memory_space=pltpu.VMEM)] * 4,
        out_specs=pl.BlockSpec(memory_space=pltpu.VMEM),
    )(group, rows, w_gate, w_up, w_down)


def spread_sum(parts, table, groups, quads, pairs, tokens, slots):
    there, features = parts.shape
    here = quads * tokens

    def body(x_ref, t_ref, o_ref):
        hot = one_hot(t_ref[...], True, groups, quads, pairs, tokens, slots)
        o_ref[...] = jnp.dot(hot, x_ref[...], preferred_element_type=F32).astype(BF)

    return call(
        body,
        jax.ShapeDtypeStruct((here, features), BF),
        in_specs=[pl.BlockSpec(memory_space=pltpu.VMEM)] * 2,
        out_specs=pl.BlockSpec(memory_space=pltpu.VMEM),
    )(parts, table)


def finish_layer(parts, hidden):
    count, tokens, features = parts.shape

    def body(x_ref, h_ref, o_ref):
        total = h_ref[...].astype(F32)
        for s in range(count):
            total = total + x_ref[s].astype(F32)
        o_ref[...] = total.astype(BF)

    return call(
        body,
        jax.ShapeDtypeStruct((tokens, features), BF),
        in_specs=[pl.BlockSpec(memory_space=pltpu.VMEM)] * 2,
        out_specs=pl.BlockSpec(memory_space=pltpu.VMEM),
    )(parts, hidden)


def on_device(
    attn_heads, out_proj, residual_in, norm_gain, expert_ids, gate_weights, w_gate, w_up, w_down
):
    tokens, features = residual_in.shape
    groups, quads, pairs = (lax.axis_size(a) for a in ("group", "quad", "pair"))
    experts = groups * w_gate.shape[0]
    slots = 3 * tokens // 4
    near, far = ("group", "pair"), "quad"
    wide = features + LANES

    partial = project(attn_heads, out_proj, groups, quads, pairs, tokens)
    arrived = exchange(partial.reshape(groups * pairs, quads * tokens, features), near)
    summed = sum_blocks(arrived)
    arrived = exchange(summed.reshape(quads, tokens, features), far)
    hidden, sent = finish_hidden(
        arrived, residual_in, norm_gain.reshape(1, features), expert_ids, gate_weights, quads, experts
    )
    seen = exchange(sent, far).reshape(quads * tokens, wide)
    picked, table = pick_rows(seen, groups, quads, pairs, tokens, slots)
    rows = exchange(picked.reshape(groups * pairs, quads * slots, wide), near)
    group = lax.axis_index("group").astype(jnp.int32).reshape(1)
    blocks = experts_of(rows.reshape(-1, wide), w_gate, w_up, w_down, group)
    back = exchange(blocks.reshape(groups * pairs, quads * slots, features), near)
    mixed = spread_sum(back.reshape(-1, features), table, groups, quads, pairs, tokens, slots)
    arrived = exchange(mixed.reshape(quads, tokens, features), far)
    return finish_layer(arrived, hidden)


def solution(mesh):
    dp, groups, tensors = mesh.devices.shape
    split = Mesh(
        mesh.devices.reshape(dp, groups, tensors // 2, 2), ("dp", "group", "quad", "pair")
    )
    inner = ("group", "quad", "pair")
    rows = P(("dp", *inner), None)
    placed = (
        P("dp", inner),
        P(inner, None),
        rows,
        P(),
        rows,
        rows,
        P("group", None, ("quad", "pair")),
        P("group", None, ("quad", "pair")),
        P("group", ("quad", "pair"), None),
    )
    return jax.shard_map(
        on_device, mesh=split, in_specs=placed, out_specs=rows, check_vma=False
    )
```

```python
import jax
import jax.numpy as jnp
from jax import lax
from jax.experimental import pallas as pl
from jax.experimental.pallas import tpu as pltpu
from jax.sharding import PartitionSpec as P

BF = jnp.bfloat16
F32 = jnp.float32
LANES = 128


def whole(shape):
    return pl.BlockSpec(shape, lambda *_: (0,) * len(shape))


def call(body, outs, grid=None, in_specs=None, out_specs=None, scratch=(), vmem=20 << 20):
    return pl.pallas_call(
        body,
        out_shape=outs,
        grid=grid if grid is not None else (),
        in_specs=in_specs,
        out_specs=out_specs,
        scratch_shapes=scratch,
        compiler_params=pltpu.CompilerParams(vmem_limit_bytes=vmem),
    )


EVERYONE = ("dp", "group", "tensor")


def exchange(blocks, lists):
    return lax.all_to_all(blocks, EVERYONE, 0, 0, axis_index_groups=lists, tiled=True)


def owner_of(core, x, yh, yl, xs, ys):
    return x * ys + (2 * yh + yl + 0 * core) % ys


def pair_groups(dps, xs, ys):
    near, far = [], []
    for dp in range(dps):
        at = lambda x, yh, yl: dp * xs * ys + owner_of(dp % 2, x, yh, yl, xs, ys)
        near += [[at(x, yh, yl) for x in range(xs) for yl in range(2)] for yh in range(ys // 2)]
        far += [[at(x, yh, yl) for yh in range(ys // 2)] for x in range(xs) for yl in range(2)]
    return near, far


def project(core, attn, weight, xs, ys, tokens):
    rows, depth = attn.shape
    features = weight.shape[1]
    width = 512
    chunks = features // width
    order = [
        (x, yh, yl) for x in range(xs) for yl in range(2) for yh in range(ys // 2)
    ]

    def body(c_ref, a_hbm, w_hbm, o_ref, a_ref, p_ref, w_ref, a_sem, w_sem):
        a_copy = pltpu.make_async_copy(a_hbm, a_ref, a_sem)
        copies = [
            pltpu.make_async_copy(
                w_hbm.at[:, pl.ds(j * width, width)], w_ref.at[j], w_sem.at[j]
            )
            for j in range(chunks)
        ]
        a_copy.start()
        for copy in copies:
            copy.start()
        core = c_ref[0]

        @pl.when(core == 1)
        def _():
            pl.delay(14000)

        a_copy.wait()
        for place, at in enumerate(order):
            src = pl.multiple_of(owner_of(core, *at, xs, ys) * tokens, tokens)
            p_ref[place * tokens : (place + 1) * tokens, :] = a_ref[pl.ds(src, tokens), :]
        for j, copy in enumerate(copies):
            copy.wait()
            o_ref[:, j * width : (j + 1) * width] = jnp.dot(
                p_ref[...], w_ref[j], preferred_element_type=F32
            ).astype(BF)

    return call(
        body,
        jax.ShapeDtypeStruct((rows, features), BF),
        in_specs=[
            pl.BlockSpec(memory_space=pltpu.SMEM),
            pl.BlockSpec(memory_space=pltpu.HBM),
            pl.BlockSpec(memory_space=pltpu.HBM),
        ],
        out_specs=pl.BlockSpec(memory_space=pltpu.VMEM),
        scratch=[
            pltpu.VMEM((rows, depth), BF),
            pltpu.VMEM((rows, depth), BF),
            pltpu.VMEM((chunks, depth, width), BF),
            pltpu.SemaphoreType.DMA,
            pltpu.SemaphoreType.DMA((chunks,)),
        ],
    )(core, pltpu.with_memory_space_constraint(attn, pltpu.HBM), pltpu.with_memory_space_constraint(weight, pltpu.HBM))


def sum_blocks(blocks, ahead):
    count, rows, features = blocks.shape

    def body(x_ref, _, o_ref):
        total = x_ref[0].astype(F32)
        for s in range(1, count):
            total = total + x_ref[s].astype(F32)
        o_ref[...] = total.astype(BF)

    return call(
        body,
        jax.ShapeDtypeStruct((rows, features), BF),
        in_specs=[pl.BlockSpec(memory_space=pltpu.VMEM)] * 2,
        out_specs=pl.BlockSpec(memory_space=pltpu.VMEM),
    )(blocks, ahead)


def finish_hidden(parts, residual, gain, ids, gates, copies, ahead):
    count, tokens, features = parts.shape

    def body(x_ref, r_ref, g_ref, id_ref, w_ref, _, h_ref, o_ref):
        total = x_ref[0].astype(F32)
        for s in range(1, count):
            total = total + x_ref[s].astype(F32)
        projected = total.astype(BF).astype(F32)
        hidden = (r_ref[...].astype(F32) + projected).astype(BF)
        h_ref[...] = hidden
        stream = hidden.astype(F32)
        scale = lax.rsqrt(jnp.mean(stream * stream, axis=1, keepdims=True) + 1e-06)
        normed = (stream * scale * g_ref[...].reshape(1, features)).astype(BF)
        lane = lax.broadcasted_iota(jnp.int32, (tokens, LANES), 1)
        table = jnp.zeros((tokens, LANES), F32)
        a = lax.broadcasted_iota(jnp.int32, (tokens, tokens), 0)
        b = lax.broadcasted_iota(jnp.int32, (tokens, tokens), 1)
        turn = jnp.where(a == b, 1.0, 0.0).astype(BF)
        nt = (((1,), (1,)), ((), ()))
        picks = lax.dot_general(
            turn, id_ref[...].astype(F32).astype(BF), nt, preferred_element_type=F32
        ).astype(jnp.int32)
        gate = lax.dot_general(turn, w_ref[...], nt, preferred_element_type=F32)
        for k in range(picks.shape[1]):
            table = table + jnp.where(lane == picks[:, k : k + 1], gate[:, k : k + 1], 0.0)
        table = table.astype(BF)
        for s in range(copies):
            o_ref[s, :, :features] = normed
            o_ref[s, :, features:] = table

    return call(
        body,
        (
            jax.ShapeDtypeStruct((tokens, features), BF),
            jax.ShapeDtypeStruct((copies, tokens, features + LANES), BF),
        ),
        in_specs=[pl.BlockSpec(memory_space=pltpu.VMEM)] * 6,
        out_specs=(pl.BlockSpec(memory_space=pltpu.VMEM),) * 2,
    )(parts, residual, gain, ids, gates, ahead)


def slot_of(index, slots):
    block = (index * 171) >> 10 if slots == 6 else index // slots
    return block, index - block * slots


def one_hot(table, table_first, groups, quads, repeat, tokens, slots):
    here = quads * tokens
    there = groups * repeat * quads * slots
    members = 2

    def split(index):
        block, slot = slot_of(index, slots)
        quad = block % quads
        group = block // (quads * repeat)
        return group, quad, slot

    group_e, _, _ = split(lax.broadcasted_iota(jnp.int32, (there, LANES), 0))
    expert = lax.broadcasted_iota(jnp.int32, (there, LANES), 1)
    belongs = (expert // members == group_e).astype(BF)
    shape = (here, there) if table_first else (there, here)
    t_dim, s_dim = (0, 1) if table_first else (1, 0)
    nt = (((1,), (1,)), ((), ()))
    pair = (table, belongs) if table_first else (belongs, table)
    chosen = lax.dot_general(*pair, nt, preferred_element_type=F32) > 0
    chosen = jnp.where(chosen, 1.0, 0.0)
    a = lax.broadcasted_iota(jnp.int32, (here, here), 0)
    b = lax.broadcasted_iota(jnp.int32, (here, here), 1)
    row, col = (a, b) if table_first else (b, a)
    before = jnp.where((row // tokens == col // tokens) & (col < row), 1.0, 0.0).astype(BF)
    flag = chosen.astype(BF)
    if table_first:
        position = jnp.dot(before, flag, preferred_element_type=F32)
    else:
        position = jnp.dot(flag, before, preferred_element_type=F32)
    _, quad, slot = split(lax.broadcasted_iota(jnp.int32, shape, s_dim))
    token = lax.broadcasted_iota(jnp.int32, shape, t_dim)
    hit = (token // tokens == quad) & (position == slot.astype(F32))
    return jnp.where(hit, chosen, 0.0).astype(BF)


def pick_rows(seen, groups, quads, pairs, tokens, slots, ahead, group):
    here, wide = seen.shape
    features = wide - LANES
    span = quads * slots

    def body(_, x_ref, __, o_ref, t_ref):
        table = x_ref[:, features:]
        t_ref[...] = table
        hot = one_hot(table, False, groups, quads, 1, tokens, slots)
        picked = jnp.dot(hot, x_ref[...], preferred_element_type=F32).astype(BF)
        for g in range(groups):
            for p in range(pairs):
                at = (g * pairs + p) * span
                o_ref[at : at + span, :] = picked[g * span : (g + 1) * span, :]

    return call(
        body,
        (
            jax.ShapeDtypeStruct((groups * pairs * span, wide), BF),
            jax.ShapeDtypeStruct((here, LANES), BF),
        ),
        in_specs=[pl.BlockSpec(memory_space=pltpu.SMEM)]
        + [pl.BlockSpec(memory_space=pltpu.VMEM)] * 2,
        out_specs=(pl.BlockSpec(memory_space=pltpu.VMEM),) * 2,
    )(group, seen, ahead)


def experts_of(rows, w_gate, w_up, w_down, group):
    count, wide = rows.shape
    features = wide - LANES
    members, _, units = w_gate.shape

    def body(g_ref, x_ref, wg_ref, wu_ref, wd_ref, o_ref):
        table = x_ref[:, features:].astype(F32)
        lane = lax.broadcasted_iota(jnp.int32, (count, LANES), 1)
        x = x_ref[:, :features]
        acts = []
        for m in range(members):
            gate = jnp.dot(x, wg_ref[m], preferred_element_type=F32)
            up = jnp.dot(x, wu_ref[m], preferred_element_type=F32)
            act = (gate / (1.0 + jnp.exp(-gate)) * up).astype(BF)
            acts.append(act)
        weights = [
            jnp.sum(jnp.where(lane == g_ref[0] * members + m, table, 0.0), axis=1, keepdims=True)
            for m in range(members)
        ]
        step = 512
        for at in range(0, features, step):
            total = jnp.zeros((count, step), F32)
            for m in range(members):
                total = total + weights[m] * jnp.dot(
                    acts[m], wd_ref[m, :, at : at + step], preferred_element_type=F32
                )
            o_ref[:, at : at + step] = total.astype(BF)

    return call(
        body,
        jax.ShapeDtypeStruct((count, features), BF),
        in_specs=[pl.BlockSpec(memory_space=pltpu.SMEM)]
        + [pl.BlockSpec(memory_space=pltpu.VMEM)] * 4,
        out_specs=pl.BlockSpec(memory_space=pltpu.VMEM),
    )(group, rows, w_gate, w_up, w_down)


def spread_sum(parts, table, groups, quads, pairs, tokens, slots):
    there, features = parts.shape
    here = quads * tokens

    def body(x_ref, t_ref, o_ref):
        hot = one_hot(t_ref[...], True, groups, quads, pairs, tokens, slots)
        o_ref[...] = jnp.dot(hot, x_ref[...], preferred_element_type=F32).astype(BF)

    return call(
        body,
        jax.ShapeDtypeStruct((here, features), BF),
        in_specs=[pl.BlockSpec(memory_space=pltpu.VMEM)] * 2,
        out_specs=pl.BlockSpec(memory_space=pltpu.VMEM),
    )(parts, table)


def finish_layer(parts, hidden):
    count, tokens, features = parts.shape

    def body(x_ref, h_ref, o_ref):
        total = h_ref[...].astype(F32)
        for s in range(count):
            total = total + x_ref[s].astype(F32)
        o_ref[...] = total.astype(BF)

    return call(
        body,
        jax.ShapeDtypeStruct((tokens, features), BF),
        in_specs=[pl.BlockSpec(memory_space=pltpu.VMEM)] * 2,
        out_specs=pl.BlockSpec(memory_space=pltpu.VMEM),
    )(parts, hidden)


def on_device(
    attn_heads, out_proj, residual_in, norm_gain, expert_ids, gate_weights, w_gate, w_up, w_down
):
    tokens, features = residual_in.shape
    groups, tensors = lax.axis_size("group"), lax.axis_size("tensor")
    quads, pairs = tensors // 2, 2
    slots = 3 * tokens // 4
    near, far = pair_groups(lax.axis_size("dp"), groups, tensors)
    wide = features + LANES
    core = (lax.axis_index("dp") % 2).astype(jnp.int32).reshape(1)
    group = lax.axis_index("group").astype(jnp.int32).reshape(1)
    core, group = lax.optimization_barrier((core, group))
    partial = project(core, attn_heads, out_proj, groups, tensors, tokens)
    arrived = exchange(partial.reshape(groups * pairs, quads * tokens, features), near)
    summed = sum_blocks(arrived, w_gate)
    arrived = exchange(summed.reshape(quads, tokens, features), far)
    hidden, sent = finish_hidden(
        arrived, residual_in, norm_gain, expert_ids.T, gate_weights.T, quads, w_up
    )
    seen = exchange(sent, far).reshape(quads * tokens, wide)
    picked, table = pick_rows(seen, groups, quads, pairs, tokens, slots, w_down, group)
    rows = exchange(picked.reshape(groups * pairs, quads * slots, wide), near)
    blocks = experts_of(rows.reshape(-1, wide), w_gate, w_up, w_down, group)
    back = exchange(blocks.reshape(groups * pairs, quads * slots, features), near)
    mixed = spread_sum(back.reshape(-1, features), table, groups, quads, pairs, tokens, slots)
    arrived = exchange(mixed.reshape(quads, tokens, features), far)
    return finish_layer(arrived, hidden)


def solution(mesh):
    inner = ("group", "tensor")
    rows = P(("dp", *inner), None)
    placed = (
        P("dp", inner),
        P(inner, None),
        rows,
        P(),
        rows,
        rows,
        P("group", None, "tensor"),
        P("group", None, "tensor"),
        P("group", "tensor", None),
    )
    return jax.shard_map(
        on_device, mesh=mesh, in_specs=placed, out_specs=rows, check_vma=False
    )
```
